32 devices in a mesh: seq: 8 (over z, y), blk: 4 (over x, core).
Axes of the slice: x: 2, y: 2, z: 4, core: 2. Of those that a mesh axis runs over, the one named last changes fastest.
Arguments:
- q_latent: bfloat16 [64, 128, 512], P('blk', 'seq'), may hold values from -16 to 16
- q_rope: bfloat16 [64, 64, 128], P('blk', None, 'seq'), may hold values from -9 to 9
- cache_latent: bfloat16 [16384, 512], P(('seq', 'blk')), may hold values from -8 to 8
- cache_rope: bfloat16 [64, 16384], P(None, ('seq', 'blk')), may hold values from -6 to 6
- draft_latent: bfloat16 [64, 512], replicated, may hold values from -8 to 8
- draft_rope: bfloat16 [64, 64], replicated, may hold values from -6 to 6
- ancestors: int32 [64, 64], replicated, may hold values from 0 to 1, as said below
- valid_length: int32 [], replicated, may hold values from 8192 to 16384
- accepted: int32 [64], P('blk'), may hold values from 0 to 1, as said below
- w_value: bfloat16 [128, 512, 128], P('seq'), may hold values from -3 to 3
Outputs:
- attended: bfloat16 [64, 128, 128], P('blk', 'seq')
- accepted_total: int32 [], replicated
The draws below stay inside these ranges and needn't reach their ends.
Inputs may be any that keep to these rules, and one draw needn't show every extreme that they name: Node 0 is the root; every other node's parent has a lower index; ancestors[i, j] = 1 exactly when j is i or an ancestor of i. accepted is the row of ancestors of one node of the tree: that node and all of its ancestors.
All inputs are finite; a program needn't handle non-finite values.
Results may differ from the reference program's by a relative error of at most 0.02.
Values may be sent and summed in bfloat16 or wider, within the bound.
A program may use at most 64 MiB of HBM per device.

```python
import jax
import jax.numpy as jnp
from jax import lax

HEADS = 128
LATENT = 512
ROPE = 64
VDIM = 128
DRAFT = 64
CACHE = 16384
N_BLK = 4


def shared_latents(key):
    base_key = jax.random.fold_in(key, 7)
    k_cache, k_query = jax.random.split(base_key, 2)
    cache = jnp.clip(jax.random.normal(k_cache, (CACHE, LATENT), jnp.float32), -6.0, 6.0)
    query = jnp.clip(1.5 * jax.random.normal(k_query, (DRAFT, HEADS, LATENT), jnp.float32), -9.0, 9.0)
    return (cache, query)


def draw_cache_latent(key, part):
    return shared_latents(key)[0].astype(jnp.bfloat16)


def draw_q_latent(key, part):
    return shared_latents(key)[1].astype(jnp.bfloat16)


def tree_tables(key):
    base_key = jax.random.fold_in(key, 13)
    k_parent, k_pick = jax.random.split(base_key)
    step = max(DRAFT // N_BLK, 1)
    nodes = jnp.arange(DRAFT, dtype=jnp.int32)
    lowest = jnp.maximum(nodes - step, 0)
    parent = jax.random.randint(k_parent, (DRAFT,), lowest, jnp.maximum(nodes, 1))
    identity = jnp.eye(DRAFT, dtype=jnp.int32)

    def extend(index, table):
        row = jnp.maximum(table[parent[index]], identity[index])
        return table.at[index].set(jnp.where(index > 0, row, identity[index]))
    table = lax.fori_loop(0, DRAFT, extend, identity)
    chosen = jax.random.randint(k_pick, (), DRAFT - step, DRAFT)
    return (table, table[chosen])


def draw_ancestors(key, part):
    return tree_tables(key)[0].astype(jnp.int32)


def draw_accepted(key, part):
    return tree_tables(key)[1].astype(jnp.int32)


def level_of(own_key, extent, cuts, smallest, top_value):
    factor_of, own = 1.0, jax.random.fold_in(own_key, 6)
    for dim, blocks in cuts:
        draws = jnp.exp(jax.random.uniform(jax.random.fold_in(own, dim), (blocks,), jnp.float32, smallest / len(cuts), top_value / len(cuts)))
        factor_of = factor_of * jnp.repeat(draws, extent[dim] // blocks).reshape([-1 if axis == dim else 1 for axis in range(len(extent))])
    return factor_of


def normal_values(rng, extent, scale, bound, cuts=(), kind=jnp.bfloat16):
    entries = scale * jax.random.normal(rng, extent, jnp.float32)
    if cuts:
        entries = entries * level_of(rng, extent, cuts, -0.22, 0.18)
    return jnp.clip(entries, -bound, bound).astype(kind)


def setup_inputs(seed: int = 0) -> dict:
    key_list = jax.random.split(jax.random.key(seed), 11)
    q_latent = draw_q_latent(jax.random.fold_in(key_list[10], 71), 0)
    q_rope = normal_values(key_list[1], (DRAFT, ROPE, HEADS), 1.5, 9.0, ((0, 4), (2, 8)))
    cache_latent = draw_cache_latent(jax.random.fold_in(key_list[10], 71), 0)
    cache_rope = normal_values(key_list[3], (ROPE, CACHE), 1.0, 6.0, ((1, 32),))
    draft_latent = normal_values(key_list[4], (DRAFT, LATENT), 1.3, 8.0)
    draft_rope = normal_values(key_list[5], (ROPE, DRAFT), 1.0, 6.0)
    ancestors = draw_ancestors(jax.random.fold_in(key_list[10], 71), 0)
    valid_length = jax.random.randint(key_list[7], (), CACHE // 2, CACHE + 1).astype(jnp.int32)
    accepted = draw_accepted(jax.random.fold_in(key_list[10], 71), 0)
    w_value = normal_values(key_list[9], (HEADS, LATENT, VDIM), 0.5, 3.0, ((0, 8),))
    return dict(q_latent=q_latent, q_rope=q_rope, cache_latent=cache_latent, cache_rope=cache_rope, draft_latent=draft_latent, draft_rope=draft_rope, ancestors=ancestors, valid_length=valid_length, accepted=accepted, w_value=w_value)


def reference(q_latent, q_rope, cache_latent, cache_rope, draft_latent, draft_rope, ancestors, valid_length, accepted, w_value):
    scale = (VDIM + ROPE) ** -0.5
    keys = cache_latent.astype(jnp.float32)
    rotary = cache_rope.astype(jnp.float32)
    draft_keys = draft_latent.astype(jnp.float32)
    draft_rot = draft_rope.astype(jnp.float32)
    live = jnp.arange(CACHE, dtype=jnp.int32) < valid_length
    tree = ancestors == 1
    width = min(8, HEADS)
    blocks = HEADS // width
    high = lax.Precision.HIGHEST

    def one_block(index):
        first = (index * width).astype(jnp.int32)
        query = lax.dynamic_slice_in_dim(q_latent, first, width, 1).astype(jnp.float32)
        qrot = lax.dynamic_slice_in_dim(q_rope, first, width, 2).astype(jnp.float32)
        weight = lax.dynamic_slice_in_dim(w_value, first, width, 0).astype(jnp.float32)
        cache_score = jnp.einsum("thl,sl->ths", query, keys, precision=high)
        cache_score = (cache_score + jnp.einsum("trh,rs->ths", qrot, rotary, precision=high)) * scale
        cache_score = jnp.where(live[None, None, :], cache_score, -1e30)
        draft_score = jnp.einsum("thl,jl->thj", query, draft_keys, precision=high)
        draft_score = (draft_score + jnp.einsum("trh,rj->thj", qrot, draft_rot, precision=high)) * scale
        draft_score = jnp.where(tree[:, None, :], draft_score, -1e30)
        peak = jnp.maximum(jnp.max(cache_score, axis=2), jnp.max(draft_score, axis=2))
        cache_w = jnp.exp(cache_score - peak[:, :, None])
        draft_w = jnp.exp(draft_score - peak[:, :, None])
        total = jnp.sum(cache_w, axis=2) + jnp.sum(draft_w, axis=2)
        latent_out = jnp.einsum("ths,sl->thl", cache_w, keys, precision=high)
        latent_out = latent_out + jnp.einsum("thj,jl->thl", draft_w, draft_keys, precision=high)
        latent_out = latent_out / total[:, :, None]
        return jnp.einsum("thl,hlv->thv", latent_out, weight, precision=high)

    stacked = lax.map(one_block, jnp.arange(blocks, dtype=jnp.int32))
    attended = jnp.transpose(stacked, (1, 0, 2, 3)).reshape(DRAFT, HEADS, VDIM)
    accepted_total = jnp.sum(accepted).astype(jnp.int32)
    return attended.astype(jnp.bfloat16), accepted_total
```

```python
import functools

import jax
import jax.numpy as jnp
from jax import lax
from jax.experimental import pallas as pl
from jax.experimental.pallas import tpu as pltpu
from jax.sharding import PartitionSpec as P

ROPE = 64
VDIM = 128
NEG = -1e30
F32 = jnp.float32
BF16 = jnp.bfloat16
NT = (((1,), (1,)), ((), ()))


def inner_extent(n_seq):
    side = 1
    while 2 * side * side * 4 <= n_seq:
        side *= 2
    return side if n_seq % side == 0 else 1


def kernel(
    nz,
    ny,
    nb,
    tokens,
    heads,
    valid_ref,
    accepted_ref,
    q_ref,
    qr_ref,
    kl_ref,
    kr_ref,
    dl_ref,
    dr_ref,
    anc_ref,
    w_ref,
    out_ref,
    count_ref,
    kbuf,
    qbuf,
    qrbuf,
    wbuf,
    top,
    tot,
    acc,
    xbuf,
    outf,
    osend,
    ssend,
    orecv,
    srecv,
    local_sem,
    qsend_sem,
    qrecv_sem,
    up_sem,
    down_sem,
    side_sem,
    recv_sem,
    xsend_sem,
    xrecv_sem,
):
    scale = (VDIM + ROPE) ** (-0.5)
    rows = tokens * heads
    keys, latent = kl_ref.shape
    seq = lax.axis_index("seq")
    blk = lax.axis_index("blk")
    z, y = seq // ny, seq % ny

    fills = [
        pltpu.make_async_copy(kl_ref, kbuf.at[seq, pl.ds(0, keys)], local_sem.at[0]),
        pltpu.make_async_copy(kr_ref, kbuf.at[seq, pl.ds(keys, ROPE)], local_sem.at[1]),
        pltpu.make_async_copy(q_ref, qbuf.at[blk], local_sem.at[2]),
        pltpu.make_async_copy(qr_ref, qrbuf.at[blk], local_sem.at[3]),
        pltpu.make_async_copy(w_ref, wbuf, local_sem.at[4]),
    ]
    for fill in fills:
        fill.start()

    def blk_peer(k):
        return {"blk": lax.rem(blk + k, nb)}

    def side_peer(j):
        return {"seq": z * ny + lax.rem(y + j, ny)}

    barrier = pltpu.get_barrier_semaphore()
    for k in range(1, nb):
        pl.semaphore_signal(barrier, inc=1, device_id=blk_peer(k))
    for j in range(1, ny):
        pl.semaphore_signal(barrier, inc=1, device_id=side_peer(j))

    @pl.when(z < nz - 1)
    def _():
        pl.semaphore_signal(barrier, inc=1, device_id={"seq": seq + ny})

    @pl.when(z > 0)
    def _():
        pl.semaphore_signal(barrier, inc=1, device_id={"seq": seq - ny})

    arrivals = (nb - 1) + (ny - 1) + jnp.where(z < nz - 1, 1, 0) + jnp.where(z > 0, 1, 0)
    pl.semaphore_wait(barrier, arrivals)

    above, below = nz - 1 - z, z
    near = jnp.minimum(above, below)

    def plane(k):
        odd = lax.rem(k, 2)
        close = jnp.where(odd == 1, z + (k + 1) // 2, z - k // 2)
        far = jnp.where(above > below, z + (k - near), z - (k - near))
        return jnp.where(k <= 2 * near, close, far)

    def remote(src, dst, send, recv, where):
        return pltpu.make_async_remote_copy(
            src_ref=src, dst_ref=dst, send_sem=send, recv_sem=recv,
            device_id=where, device_id_type=pl.DeviceIdType.MESH,
        )

    def piece(p, send, where):
        return remote(kbuf.at[p], kbuf.at[p], send, recv_sem.at[p], where)

    def up(k):
        return piece(plane(k) * ny + y, up_sem.at[k], {"seq": jnp.minimum(seq + ny, nz * ny - 1)})

    def down(k):
        return piece(plane(k) * ny + y, down_sem.at[k], {"seq": jnp.maximum(seq - ny, 0)})

    def side(k, j):
        return piece(plane(k) * ny + y, side_sem.at[k * max(ny - 1, 1) + j - 1], side_peer(j))

    def sends(k, act):
        @pl.when(jnp.logical_and(plane(k) <= z, z < nz - 1))
        def _():
            act(up(k))

        @pl.when(jnp.logical_and(plane(k) >= z, z > 0))
        def _():
            act(down(k))

        for j in range(1, ny):
            act(side(k, j))

    fills[0].wait()
    fills[1].wait()
    sends(0, lambda c: c.start())

    def query_copies(k):
        return (
            remote(q_ref, qbuf.at[blk], qsend_sem.at[2 * k - 2], qrecv_sem.at[2 * k - 2], blk_peer(k)),
            remote(qr_ref, qrbuf.at[blk], qsend_sem.at[2 * k - 1], qrecv_sem.at[2 * k - 1], blk_peer(k)),
        )

    for k in range(1, nb):
        for c in query_copies(k):
            c.start()

    top[...] = jnp.full_like(top, NEG)
    tot[...] = jnp.zeros_like(tot)

    def clear(i, carry):
        acc[pl.ds(i * rows, rows), :] = jnp.zeros((rows, latent), F32)
        return carry

    lax.fori_loop(0, nb, clear, 0)
    fills[2].wait()
    fills[3].wait()
    nodes = dl_ref.shape[0]
    dscore = lax.dot_general(qbuf[blk], dl_ref[...], NT, preferred_element_type=F32)
    dscore = dscore + jnp.dot(qrbuf[blk], dr_ref[...], preferred_element_type=F32)
    row = lax.broadcasted_iota(jnp.int32, (rows, tokens), 0)
    first = lax.broadcasted_iota(jnp.int32, (rows, tokens), 1) * heads
    spread = jnp.where(jnp.logical_and(row >= first, row < first + heads), 1.0, 0.0)
    tree = anc_ref[pl.ds(pl.multiple_of(blk * tokens, tokens), tokens), :].astype(F32)
    tree = jnp.dot(spread, tree, preferred_element_type=F32)
    dscore = jnp.where(tree > 0.5, dscore * scale, NEG)
    dpeak = jnp.max(dscore, axis=1, keepdims=True)
    dweight = jnp.exp(dscore - dpeak)
    top[blk] = dpeak
    tot[blk] = jnp.sum(dweight, axis=1, keepdims=True)
    acc[pl.ds(pl.multiple_of(blk * rows, rows), rows), :] = jnp.dot(
        dweight.astype(BF16), dl_ref[...], preferred_element_type=F32
    )
    valid = valid_ref[0]

    def attend(p):
        start = (p * nb + blk) * keys
        live = start + lax.broadcasted_iota(jnp.int32, (1, keys), 1) < valid

        def block(i, carry):
            key = kbuf[p, pl.ds(0, keys), :]
            score = lax.dot_general(qbuf[i], key, NT, preferred_element_type=F32)
            score = score + jnp.dot(
                qrbuf[i], kbuf[p, pl.ds(keys, ROPE), :], preferred_element_type=F32
            )
            score = jnp.where(live, score * scale, NEG)
            old = top[i]
            new = jnp.maximum(old, jnp.max(score, axis=1, keepdims=True))
            weight = jnp.exp(score - new)
            fade = jnp.exp(old - new)
            top[i] = new
            tot[i] = tot[i] * fade + jnp.sum(weight, axis=1, keepdims=True)
            at = pl.ds(pl.multiple_of(i * rows, rows), rows)
            acc[at, :] = acc[at, :] * fade + jnp.dot(
                weight.astype(BF16), key, preferred_element_type=F32
            )
            return carry

        lax.fori_loop(0, nb, block, 0)

    def step(k, carry):
        @pl.when(jnp.logical_and(k >= 1, k < nz))
        def _():
            p = plane(k) * ny + y
            piece(p, recv_sem.at[p], {"seq": seq}).wait_recv()
            sends(k, lambda c: c.start())

        @pl.when(k == 1)
        def _():
            for j in range(1, nb):
                for c in query_copies(j):
                    c.wait_recv()

        @pl.when(k <= nz)
        def _():
            attend(plane(k - 1) * ny + y)

        @pl.when(k >= 2)
        def _():
            def one(j, inner):
                p = plane(k - 2) * ny + lax.rem(y + j, ny)
                piece(p, recv_sem.at[p], {"seq": seq}).wait_recv()
                attend(p)
                return inner

            lax.fori_loop(1, ny, one, 0)

        return carry

    lax.fori_loop(1, nz + 2, step, 0)

    def finish(i, carry):
        at = pl.ds(pl.multiple_of(i * rows, rows), rows)
        scaled = acc[at, :] / tot[i]
        for c in range(latent // 128):
            xbuf[c, at, :] = scaled[:, c * 128 : (c + 1) * 128]
        lse = top[i] + jnp.log(tot[i])
        flat = jnp.transpose(jnp.broadcast_to(lse, (rows, 128)))
        ssend[i, pl.ds(0, 8), :] = flat[0:8]
        return carry

    lax.fori_loop(0, nb, finish, 0)
    fills[4].wait()
    for h in range(heads):
        x = jnp.concatenate(
            [
                xbuf.at[c][pl.ds(h, nb * tokens, stride=heads), :]
                for c in range(latent // 128)
            ],
            axis=1,
        ).astype(BF16)
        outf[pl.ds(h, nb * tokens, stride=heads), :] = jnp.dot(
            x, wbuf[h], preferred_element_type=F32
        )
    mine = accepted_ref[0]
    for t in range(1, tokens):
        mine = mine + accepted_ref[t]
    count = jnp.full((8, rows), mine, jnp.int32).astype(F32)
    for i in range(nb):
        osend[i] = outf[pl.ds(i * rows, rows), :].astype(BF16)
        ssend[i, pl.ds(8, 8), :] = count

    def result_copies(k):
        to = lax.rem(blk + k, nb)
        return (
            remote(osend.at[to], orecv.at[k - 1], xsend_sem.at[2 * k - 2], xrecv_sem.at[2 * k - 2], blk_peer(k)),
            remote(ssend.at[to], srecv.at[k - 1], xsend_sem.at[2 * k - 1], xrecv_sem.at[2 * k - 1], blk_peer(k)),
        )

    for k in range(1, nb):
        for c in result_copies(k):
            c.start()

    def column(flat):
        return jnp.transpose(jnp.broadcast_to(flat, (128, rows)))

    for k in range(1, nb):
        for c in result_copies(k):
            c.wait_recv()
    lses = [column(ssend[blk, pl.ds(0, 1), :])]
    lses += [column(srecv[k - 1, pl.ds(0, 1), :]) for k in range(1, nb)]
    peak = functools.reduce(jnp.maximum, lses)
    weights = [jnp.exp(v - peak) for v in lses]
    whole = functools.reduce(jnp.add, weights)
    merged = weights[0] * outf[pl.ds(pl.multiple_of(blk * rows, rows), rows), :]
    for k in range(1, nb):
        merged = merged + weights[k] * orecv[k - 1].astype(F32)
    out_ref[...] = (merged / whole).astype(out_ref.dtype)
    for k in range(1, nb):
        count = count + srecv[k - 1, pl.ds(8, 8), :]
    count_ref[...] = count[:, 0:1].astype(jnp.int32)

    def drain(k, carry):
        sends(k, lambda c: c.wait_send())
        return carry

    lax.fori_loop(0, nz, drain, 0)
    for k in range(1, nb):
        for c in query_copies(k):
            c.wait_send()
        for c in result_copies(k):
            c.wait_send()


def shards(n_seq, n_blk, q_latent, q_rope, cache_latent, cache_rope, draft_latent, draft_rope,
           ancestors, valid_length, accepted, w_value):
    tokens, heads, latent = q_latent.shape
    rows = tokens * heads
    keys = cache_latent.shape[0]
    ny = inner_extent(n_seq)
    nz = n_seq // ny
    side = max(ny - 1, 1)
    assert keys == latent
    query = q_latent.reshape(rows, latent)
    rotary = jnp.transpose(q_rope, (0, 2, 1)).reshape(rows, ROPE)
    vmem = pl.BlockSpec(memory_space=pltpu.VMEM)
    smem = pl.BlockSpec(memory_space=pltpu.SMEM)
    hbm = pl.BlockSpec(memory_space=pl.ANY)
    dma = pltpu.SemaphoreType.DMA
    out, count = pl.pallas_call(
        functools.partial(kernel, nz, ny, n_blk, tokens, heads),
        out_shape=(
            jax.ShapeDtypeStruct((rows, VDIM), BF16),
            jax.ShapeDtypeStruct((8, 1), jnp.int32),
        ),
        in_specs=[smem, smem, hbm, hbm, hbm, hbm, vmem, vmem, vmem, hbm],
        out_specs=(vmem, vmem),
        scratch_shapes=[
            pltpu.VMEM((n_seq, keys + ROPE, latent), BF16),
            pltpu.VMEM((n_blk, rows, latent), BF16),
            pltpu.VMEM((n_blk, rows, ROPE), BF16),
            pltpu.VMEM((heads, latent, VDIM), BF16),
            pltpu.VMEM((n_blk, rows, 1), F32),
            pltpu.VMEM((n_blk, rows, 1), F32),
            pltpu.VMEM((n_blk * rows, latent), F32),
            pltpu.VMEM((latent // 128, n_blk * rows, 128), F32),
            pltpu.VMEM((n_blk * rows, VDIM), F32),
            pltpu.VMEM((n_blk, rows, VDIM), BF16),
            pltpu.VMEM((n_blk, 16, rows), F32),
            pltpu.VMEM((n_blk - 1, rows, VDIM), BF16),
            pltpu.VMEM((n_blk - 1, 16, rows), F32),
            dma((5,)),
            dma((2 * (n_blk - 1),)),
            dma((2 * (n_blk - 1),)),
            dma((nz,)),
            dma((nz,)),
            dma((nz * side,)),
            dma((n_seq,)),
            dma((2 * (n_blk - 1),)),
            dma((2 * (n_blk - 1),)),
        ],
        compiler_params=pltpu.CompilerParams(
            collective_id=0, has_side_effects=True, vmem_limit_bytes=60 * 1024 * 1024
        ),
    )(
        valid_length.reshape(1), accepted, query, rotary, cache_latent, cache_rope,
        draft_latent, draft_rope, ancestors, w_value,
    )
    return (out.reshape(tokens, heads, VDIM), count[0, 0])


def solution(mesh):
    body = functools.partial(shards, mesh.shape["seq"], mesh.shape["blk"])
    return jax.shard_map(
        body,
        mesh=mesh,
        in_specs=(
            P("blk", "seq", None),
            P("blk", None, "seq"),
            P(("seq", "blk"), None),
            P(None, ("seq", "blk")),
            P(),
            P(),
            P(),
            P(),
            P("blk"),
            P("seq", None, None),
        ),
        out_specs=(P("blk", "seq", None), P()),
        check_vma=False,
    )
```

```python
import functools

import jax
import jax.numpy as jnp
from jax import lax
from jax.experimental import pallas as pl
from jax.experimental.pallas import tpu as pltpu
from jax.sharding import PartitionSpec as P

ROPE = 64
VDIM = 128
NEG = -1e30
F32 = jnp.float32
BF16 = jnp.bfloat16
NT = (((1,), (1,)), ((), ()))


def inner_extent(n_seq):
    side = 1
    while 2 * side * side * 4 <= n_seq:
        side *= 2
    return side if n_seq % side == 0 else 1


def kernel(
    nz,
    ny,
    nb,
    tokens,
    heads,
    valid_ref,
    accepted_ref,
    q_ref,
    qr_ref,
    kl_ref,
    kr_ref,
    dl_ref,
    dr_ref,
    anc_ref,
    w_ref,
    out_ref,
    count_ref,
    kbuf,
    qbuf,
    qrbuf,
    rawbuf,
    wbuf,
    top,
    tot,
    acc,
    xbuf,
    outf,
    osend,
    ssend,
    orecv,
    srecv,
    local_sem,
    qsend_sem,
    qrecv_sem,
    up_sem,
    down_sem,
    side_sem,
    recv_sem,
    xsend_sem,
    xrecv_sem,
):
    scale = (VDIM + ROPE) ** (-0.5)
    rows = tokens * heads
    keys, latent = kl_ref.shape
    seq = lax.axis_index("seq")
    blk = lax.axis_index("blk")
    z, y = seq // ny, seq % ny

    fills = [
        pltpu.make_async_copy(kl_ref, kbuf.at[seq, pl.ds(0, keys)], local_sem.at[0]),
        pltpu.make_async_copy(kr_ref, kbuf.at[seq, pl.ds(keys, ROPE)], local_sem.at[1]),
        pltpu.make_async_copy(q_ref, qbuf.at[blk], local_sem.at[2]),
        pltpu.make_async_copy(qr_ref, rawbuf, local_sem.at[3]),
        pltpu.make_async_copy(w_ref, wbuf, local_sem.at[4]),
    ]
    for fill in fills:
        fill.start()

    def blk_peer(k):
        return {"blk": lax.rem(blk + k, nb)}

    def side_peer(j):
        return {"seq": z * ny + lax.rem(y + j, ny)}

    fills[3].wait()
    turned = [jnp.transpose(rawbuf[t].astype(F32)) for t in range(tokens)]
    qrbuf[blk] = jnp.concatenate(turned, axis=0).astype(BF16)

    barrier = pltpu.get_barrier_semaphore()
    for k in range(1, nb):
        pl.semaphore_signal(barrier, inc=1, device_id=blk_peer(k))
    for j in range(1, ny):
        pl.semaphore_signal(barrier, inc=1, device_id=side_peer(j))

    @pl.when(z < nz - 1)
    def _():
        pl.semaphore_signal(barrier, inc=1, device_id={"seq": seq + ny})

    @pl.when(z > 0)
    def _():
        pl.semaphore_signal(barrier, inc=1, device_id={"seq": seq - ny})

    arrivals = (nb - 1) + (ny - 1) + jnp.where(z < nz - 1, 1, 0) + jnp.where(z > 0, 1, 0)
    pl.semaphore_wait(barrier, arrivals)

    above, below = nz - 1 - z, z
    near = jnp.minimum(above, below)

    def plane(k):
        odd = lax.rem(k, 2)
        close = jnp.where(odd == 1, z + (k + 1) // 2, z - k // 2)
        far = jnp.where(above > below, z + (k - near), z - (k - near))
        return jnp.where(k <= 2 * near, close, far)

    def remote(src, dst, send, recv, where):
        return pltpu.make_async_remote_copy(
            src_ref=src, dst_ref=dst, send_sem=send, recv_sem=recv,
            device_id=where, device_id_type=pl.DeviceIdType.MESH,
        )

    cut = (keys + ROPE) // 6 // 16 * 16
    spans = (pl.ds(0, cut), pl.ds(cut, keys + ROPE - cut))

    def slot(k, j):
        return plane(k) * ny + lax.rem(y + j, ny)

    def part(p, c, send, where):
        here = kbuf.at[p, spans[c]]
        return remote(here, here, send, recv_sem.at[2 * p + c], where)

    def arrived(p, c):
        part(p, c, recv_sem.at[2 * p + c], {"seq": seq}).wait_recv()

    def along(k, j, c, act):
        index = 2 * (k * ny + j) + c

        @pl.when(jnp.logical_and(plane(k) <= z, z < nz - 1))
        def _():
            to = {"seq": jnp.minimum(seq + ny, nz * ny - 1)}
            act(part(slot(k, j), c, up_sem.at[index], to))

        @pl.when(jnp.logical_and(plane(k) >= z, z > 0))
        def _():
            to = {"seq": jnp.maximum(seq - ny, 0)}
            act(part(slot(k, j), c, down_sem.at[index], to))

    def across(k, c, act):
        for j in range(1, ny):
            index = 2 * (k * ny + j) + c
            act(part(slot(k, 0), c, side_sem.at[index], side_peer(j)))

    def start(copy):
        copy.start()

    def wait_send(copy):
        copy.wait_send()

    fills[0].wait()
    fills[1].wait()
    for c in range(2):
        across(0, c, start)
        along(0, 0, c, start)

    def query_copies(k):
        return (
            remote(q_ref, qbuf.at[blk], qsend_sem.at[2 * k - 2], qrecv_sem.at[2 * k - 2], blk_peer(k)),
            remote(qrbuf.at[blk], qrbuf.at[blk], qsend_sem.at[2 * k - 1], qrecv_sem.at[2 * k - 1], blk_peer(k)),
        )

    for k in range(1, nb):
        for c in query_copies(k):
            c.start()

    top[...] = jnp.full_like(top, NEG)
    tot[...] = jnp.zeros_like(tot)

    def clear(i, carry):
        acc[pl.ds(i * rows, rows), :] = jnp.zeros((rows, latent), F32)
        return carry

    lax.fori_loop(0, nb, clear, 0)
    fills[2].wait()
    nodes = dl_ref.shape[0]
    dscore = lax.dot_general(qbuf[blk], dl_ref[...], NT, preferred_element_type=F32)
    dscore = dscore + jnp.dot(qrbuf[blk], dr_ref[...], preferred_element_type=F32)
    row = lax.broadcasted_iota(jnp.int32, (rows, tokens), 0)
    first = lax.broadcasted_iota(jnp.int32, (rows, tokens), 1) * heads
    spread = jnp.where(jnp.logical_and(row >= first, row < first + heads), 1.0, 0.0)
    tree = anc_ref[pl.ds(pl.multiple_of(blk * tokens, tokens), tokens), :].astype(F32)
    tree = jnp.dot(spread, tree, preferred_element_type=F32)
    dscore = jnp.where(tree > 0.5, dscore * scale, NEG)
    dpeak = jnp.max(dscore, axis=1, keepdims=True)
    dweight = jnp.exp(dscore - dpeak)
    top[blk] = dpeak
    tot[blk] = jnp.sum(dweight, axis=1, keepdims=True)
    acc[pl.ds(pl.multiple_of(blk * rows, rows), rows), :] = jnp.dot(
        dweight.astype(BF16), dl_ref[...], preferred_element_type=F32
    )
    valid = valid_ref[0]

    def attend(p):
        start = (p * nb + blk) * keys
        live = start + lax.broadcasted_iota(jnp.int32, (1, keys), 1) < valid

        def block(i, carry):
            key = kbuf[p, pl.ds(0, keys), :]
            score = lax.dot_general(qbuf[i], key, NT, preferred_element_type=F32)
            score = score + jnp.dot(
                qrbuf[i], kbuf[p, pl.ds(keys, ROPE), :], preferred_element_type=F32
            )
            score = jnp.where(live, score * scale, NEG)
            old = top[i]
            new = jnp.maximum(old, jnp.max(score, axis=1, keepdims=True))
            weight = jnp.exp(score - new)
            fade = jnp.exp(old - new)
            top[i] = new
            tot[i] = tot[i] * fade + jnp.sum(weight, axis=1, keepdims=True)
            at = pl.ds(pl.multiple_of(i * rows, rows), rows)
            acc[at, :] = acc[at, :] * fade + jnp.dot(
                weight.astype(BF16), key, preferred_element_type=F32
            )
            return carry

        lax.fori_loop(0, nb, block, 0)

    def step(k, carry):
        @pl.when(jnp.logical_and(k >= 1, k < nz))
        def _():
            arrived(slot(k, 0), 0)
            along(k, 0, 0, start)
            arrived(slot(k, 0), 1)
            along(k, 0, 1, start)
            across(k, 1, start)
            for j in range(1, ny):
                arrived(slot(k, j), 0)
                along(k, j, 0, start)

        @pl.when(k == 1)
        def _():
            for j in range(1, nb):
                for c in query_copies(j):
                    c.wait_recv()

        @pl.when(k <= nz)
        def _():
            attend(slot(k - 1, 0))

        @pl.when(k >= 2)
        def _():
            def one(j, inner):
                p = slot(k - 2, j)
                arrived(p, 1)
                attend(p)
                return inner

            lax.fori_loop(1, ny, one, 0)

        return carry

    for j in range(1, ny):
        arrived(slot(0, j), 0)
        along(0, j, 0, start)
    lax.fori_loop(1, nz + 2, step, 0)

    def finish(i, carry):
        at = pl.ds(pl.multiple_of(i * rows, rows), rows)
        scaled = acc[at, :] / tot[i]
        for c in range(latent // 128):
            xbuf[c, at, :] = scaled[:, c * 128 : (c + 1) * 128]
        lse = top[i] + jnp.log(tot[i])
        flat = jnp.transpose(jnp.broadcast_to(lse, (rows, 128)))
        ssend[i, pl.ds(0, 8), :] = flat[0:8]
        return carry

    lax.fori_loop(0, nb, finish, 0)
    fills[4].wait()
    for h in range(heads):
        x = jnp.concatenate(
            [
                xbuf.at[c][pl.ds(h, nb * tokens, stride=heads), :]
                for c in range(latent // 128)
            ],
            axis=1,
        ).astype(BF16)
        outf[pl.ds(h, nb * tokens, stride=heads), :] = jnp.dot(
            x, wbuf[h], preferred_element_type=F32
        )
    mine = accepted_ref[0]
    for t in range(1, tokens):
        mine = mine + accepted_ref[t]
    count = jnp.full((8, rows), mine, jnp.int32).astype(F32)
    for i in range(nb):
        osend[i] = outf[pl.ds(i * rows, rows), :].astype(BF16)
        ssend[i, pl.ds(8, 8), :] = count

    def result_copies(k):
        to = lax.rem(blk + k, nb)
        return (
            remote(osend.at[to], orecv.at[k - 1], xsend_sem.at[2 * k - 2], xrecv_sem.at[2 * k - 2], blk_peer(k)),
            remote(ssend.at[to], srecv.at[k - 1], xsend_sem.at[2 * k - 1], xrecv_sem.at[2 * k - 1], blk_peer(k)),
        )

    for k in range(1, nb):
        for c in result_copies(k):
            c.start()

    def column(flat):
        return jnp.transpose(jnp.broadcast_to(flat, (128, rows)))

    for k in range(1, nb):
        for c in result_copies(k):
            c.wait_recv()
    lses = [column(ssend[blk, pl.ds(0, 1), :])]
    lses += [column(srecv[k - 1, pl.ds(0, 1), :]) for k in range(1, nb)]
    peak = functools.reduce(jnp.maximum, lses)
    weights = [jnp.exp(v - peak) for v in lses]
    whole = functools.reduce(jnp.add, weights)
    merged = weights[0] * outf[pl.ds(pl.multiple_of(blk * rows, rows), rows), :]
    for k in range(1, nb):
        merged = merged + weights[k] * orecv[k - 1].astype(F32)
    out_ref[...] = (merged / whole).astype(out_ref.dtype)
    for k in range(1, nb):
        count = count + srecv[k - 1, pl.ds(8, 8), :]
    count_ref[0] = jnp.max(count).astype(jnp.int32)

    def drain(k, carry):
        along(k, 0, 0, wait_send)
        along(k, 0, 1, wait_send)
        across(k, 1, wait_send)
        for j in range(1, ny):
            along(k, j, 0, wait_send)
        return carry

    across(0, 0, wait_send)
    lax.fori_loop(0, nz, drain, 0)
    for k in range(1, nb):
        for c in query_copies(k):
            c.wait_send()
        for c in result_copies(k):
            c.wait_send()


def shards(n_seq, n_blk, q_latent, q_rope, cache_latent, cache_rope, draft_latent, draft_rope,
           ancestors, valid_length, accepted, w_value):
    tokens, heads, latent = q_latent.shape
    rows = tokens * heads
    keys = cache_latent.shape[0]
    ny = inner_extent(n_seq)
    nz = n_seq // ny
    assert keys == latent
    query = q_latent.reshape(rows, latent)
    vmem = pl.BlockSpec(memory_space=pltpu.VMEM)
    smem = pl.BlockSpec(memory_space=pltpu.SMEM)
    hbm = pl.BlockSpec(memory_space=pl.ANY)
    dma = pltpu.SemaphoreType.DMA
    out, count = pl.pallas_call(
        functools.partial(kernel, nz, ny, n_blk, tokens, heads),
        out_shape=(
            jax.ShapeDtypeStruct((rows, VDIM), BF16),
            jax.ShapeDtypeStruct((1,), jnp.int32),
        ),
        in_specs=[smem, smem, hbm, hbm, hbm, hbm, vmem, vmem, vmem, hbm],
        out_specs=(vmem, smem),
        scratch_shapes=[
            pltpu.VMEM((n_seq, keys + ROPE, latent), BF16),
            pltpu.VMEM((n_blk, rows, latent), BF16),
            pltpu.VMEM((n_blk, rows, ROPE), BF16),
            pltpu.VMEM((tokens, ROPE, heads), BF16),
            pltpu.VMEM((heads, latent, VDIM), BF16),
            pltpu.VMEM((n_blk, rows, 1), F32),
            pltpu.VMEM((n_blk, rows, 1), F32),
            pltpu.VMEM((n_blk * rows, latent), F32),
            pltpu.VMEM((latent // 128, n_blk * rows, 128), F32),
            pltpu.VMEM((n_blk * rows, VDIM), F32),
            pltpu.VMEM((n_blk, rows, VDIM), BF16),
            pltpu.VMEM((n_blk, 16, rows), F32),
            pltpu.VMEM((n_blk - 1, rows, VDIM), BF16),
            pltpu.VMEM((n_blk - 1, 16, rows), F32),
            dma((5,)),
            dma((2 * (n_blk - 1),)),
            dma((2 * (n_blk - 1),)),
            dma((2 * n_seq,)),
            dma((2 * n_seq,)),
            dma((2 * n_seq,)),
            dma((2 * n_seq,)),
            dma((2 * (n_blk - 1),)),
            dma((2 * (n_blk - 1),)),
        ],
        compiler_params=pltpu.CompilerParams(
            collective_id=0, has_side_effects=True, vmem_limit_bytes=60 * 1024 * 1024
        ),
    )(
        valid_length.reshape(1), accepted, query, q_rope, cache_latent, cache_rope,
        draft_latent, draft_rope, ancestors, w_value,
    )
    return (out.reshape(tokens, heads, VDIM), count.reshape(()))


def solution(mesh):
    body = functools.partial(shards, mesh.shape["seq"], mesh.shape["blk"])
    return jax.shard_map(
        body,
        mesh=mesh,
        in_specs=(
            P("blk", "seq", None),
            P("blk", None, "seq"),
            P(("seq", "blk"), None),
            P(None, ("seq", "blk")),
            P(),
            P(),
            P(),
            P(),
            P("blk"),
            P("seq", None, None),
        ),
        out_specs=(P("blk", "seq", None), P()),
        check_vma=False,
    )
```

```python
import functools

import jax
import jax.numpy as jnp
from jax import lax
from jax.experimental import pallas as pl
from jax.experimental.pallas import tpu as pltpu
from jax.sharding import PartitionSpec as P

ROPE = 64
VDIM = 128
PARTS = 6
NEG = -1e30
F32 = jnp.float32
BF16 = jnp.bfloat16
NT = (((1,), (1,)), ((), ()))


def inner_extent(n_seq):
    side = 1
    while 2 * side * side * 4 <= n_seq:
        side *= 2
    return side if n_seq % side == 0 else 1


def kernel(
    nz,
    ny,
    nb,
    tokens,
    heads,
    valid_ref,
    accepted_ref,
    q_ref,
    qr_ref,
    kl_ref,
    kr_ref,
    dl_ref,
    dr_ref,
    anc_ref,
    w_ref,
    out_ref,
    count_ref,
    kbuf,
    qbuf,
    qrbuf,
    rawbuf,
    wbuf,
    top,
    tot,
    acc,
    xbuf,
    outf,
    osend,
    ssend,
    orecv,
    srecv,
    local_sem,
    qsend_sem,
    qrecv_sem,
    up_sem,
    down_sem,
    side_sem,
    recv_sem,
    xsend_sem,
    xrecv_sem,
):
    scale = (VDIM + ROPE) ** (-0.5)
    rows = tokens * heads
    keys, latent = kl_ref.shape
    seq = lax.axis_index("seq")
    blk = lax.axis_index("blk")
    z, y = seq // ny, seq % ny

    fills = [
        pltpu.make_async_copy(kl_ref, kbuf.at[seq, pl.ds(0, keys)], local_sem.at[0]),
        pltpu.make_async_copy(kr_ref, kbuf.at[seq, pl.ds(keys, ROPE)], local_sem.at[1]),
        pltpu.make_async_copy(q_ref, qbuf.at[blk], local_sem.at[2]),
        pltpu.make_async_copy(qr_ref, rawbuf, local_sem.at[3]),
        pltpu.make_async_copy(w_ref, wbuf, local_sem.at[4]),
    ]
    for fill in fills:
        fill.start()

    def blk_peer(k):
        return {"blk": lax.rem(blk + k, nb)}

    def side_peer(j):
        return {"seq": z * ny + lax.rem(y + j, ny)}

    fills[3].wait()
    turned = [jnp.transpose(rawbuf[t].astype(F32)) for t in range(tokens)]
    qrbuf[blk] = jnp.concatenate(turned, axis=0).astype(BF16)

    barrier = pltpu.get_barrier_semaphore()
    for k in range(1, nb):
        pl.semaphore_signal(barrier, inc=1, device_id=blk_peer(k))
    for j in range(1, ny):
        pl.semaphore_signal(barrier, inc=1, device_id=side_peer(j))

    @pl.when(z < nz - 1)
    def _():
        pl.semaphore_signal(barrier, inc=1, device_id={"seq": seq + ny})

    @pl.when(z > 0)
    def _():
        pl.semaphore_signal(barrier, inc=1, device_id={"seq": seq - ny})

    arrivals = (nb - 1) + (ny - 1) + jnp.where(z < nz - 1, 1, 0) + jnp.where(z > 0, 1, 0)
    pl.semaphore_wait(barrier, arrivals)

    above, below = nz - 1 - z, z
    near = jnp.minimum(above, below)

    def plane(k):
        odd = lax.rem(k, 2)
        close = jnp.where(odd == 1, z + (k + 1) // 2, z - k // 2)
        far = jnp.where(above > below, z + (k - near), z - (k - near))
        return jnp.where(k <= 2 * near, close, far)

    def remote(src, dst, send, recv, where):
        return pltpu.make_async_remote_copy(
            src_ref=src, dst_ref=dst, send_sem=send, recv_sem=recv,
            device_id=where, device_id_type=pl.DeviceIdType.MESH,
        )

    size = (keys + ROPE) // PARTS

    def slot(k, j):
        return plane(k) * ny + lax.rem(y + j, ny)

    def part(p, c, send, where):
        here = kbuf.at[p, pl.ds(pl.multiple_of(c * size, 16), size)]
        return remote(here, here, send, recv_sem.at[PARTS * p + c], where)

    def arrived(p, c):
        part(p, c, recv_sem.at[PARTS * p + c], {"seq": seq}).wait_recv()

    def along(k, j, c, act):
        index = PARTS * (k * ny + j) + c

        @pl.when(jnp.logical_and(plane(k) <= z, z < nz - 1))
        def _():
            to = {"seq": jnp.minimum(seq + ny, nz * ny - 1)}
            act(part(slot(k, j), c, up_sem.at[index], to))

        @pl.when(jnp.logical_and(plane(k) >= z, z > 0))
        def _():
            to = {"seq": jnp.maximum(seq - ny, 0)}
            act(part(slot(k, j), c, down_sem.at[index], to))

    def across(k, c, act):
        for j in range(1, ny):
            index = PARTS * (k * ny + j) + c
            act(part(slot(k, 0), c, side_sem.at[index], side_peer(j)))

    def start(copy):
        copy.start()

    def wait_send(copy):
        copy.wait_send()

    fills[0].wait()
    fills[1].wait()
    for c in range(PARTS):
        across(0, c, start)
        along(0, 0, c, start)

    def query_copies(k):
        return (
            remote(q_ref, qbuf.at[blk], qsend_sem.at[2 * k - 2], qrecv_sem.at[2 * k - 2], blk_peer(k)),
            remote(qrbuf.at[blk], qrbuf.at[blk], qsend_sem.at[2 * k - 1], qrecv_sem.at[2 * k - 1], blk_peer(k)),
        )

    for k in range(1, nb):
        for c in query_copies(k):
            c.start()

    top[...] = jnp.full_like(top, NEG)
    tot[...] = jnp.zeros_like(tot)

    def clear(i, carry):
        acc[pl.ds(i * rows, rows), :] = jnp.zeros((rows, latent), F32)
        return carry

    lax.fori_loop(0, nb, clear, 0)
    fills[2].wait()
    nodes = dl_ref.shape[0]
    dscore = lax.dot_general(qbuf[blk], dl_ref[...], NT, preferred_element_type=F32)
    dscore = dscore + jnp.dot(qrbuf[blk], dr_ref[...], preferred_element_type=F32)
    row = lax.broadcasted_iota(jnp.int32, (rows, tokens), 0)
    first = lax.broadcasted_iota(jnp.int32, (rows, tokens), 1) * heads
    spread = jnp.where(jnp.logical_and(row >= first, row < first + heads), 1.0, 0.0)
    tree = anc_ref[pl.ds(pl.multiple_of(blk * tokens, tokens), tokens), :].astype(F32)
    tree = jnp.dot(spread, tree, preferred_element_type=F32)
    dscore = jnp.where(tree > 0.5, dscore * scale, NEG)
    dpeak = jnp.max(dscore, axis=1, keepdims=True)
    dweight = jnp.exp(dscore - dpeak)
    top[blk] = dpeak
    tot[blk] = jnp.sum(dweight, axis=1, keepdims=True)
    acc[pl.ds(pl.multiple_of(blk * rows, rows), rows), :] = jnp.dot(
        dweight.astype(BF16), dl_ref[...], preferred_element_type=F32
    )
    valid = valid_ref[0]

    def attend(p, low, high):
        first_key = (p * nb + blk) * keys
        live = first_key + lax.broadcasted_iota(jnp.int32, (1, keys), 1) < valid

        def block(i, carry):
            key = kbuf[p, pl.ds(0, keys), :]
            score = lax.dot_general(qbuf[i], key, NT, preferred_element_type=F32)
            score = score + jnp.dot(
                qrbuf[i], kbuf[p, pl.ds(keys, ROPE), :], preferred_element_type=F32
            )
            score = jnp.where(live, score * scale, NEG)
            old = top[i]
            new = jnp.maximum(old, jnp.max(score, axis=1, keepdims=True))
            weight = jnp.exp(score - new)
            fade = jnp.exp(old - new)
            top[i] = new
            tot[i] = tot[i] * fade + jnp.sum(weight, axis=1, keepdims=True)
            at = pl.ds(pl.multiple_of(i * rows, rows), rows)
            acc[at, :] = acc[at, :] * fade + jnp.dot(
                weight.astype(BF16), key, preferred_element_type=F32
            )
            return carry

        lax.fori_loop(low, high, block, 0)

    def step(k, carry):
        def turn(c, inner):
            @pl.when(k < nz)
            def _():
                arrived(slot(k, 0), c)
                along(k, 0, c, start)

                @pl.when(c > 0)
                def _():
                    across(k, c, start)

            low, high = c * nb // PARTS, (c + 1) * nb // PARTS

            @pl.when(jnp.logical_and(k >= 2, c == 0))
            def _():
                for j in range(1, ny):
                    for other in range(1, PARTS):
                        arrived(slot(k - 2, j), other)

            def own_line(n, x):
                attend(slot(jnp.where(n == 0, 0, k - 1), 0), low, high)
                return x

            lax.fori_loop(
                jnp.where(k == 2, 0, 1), jnp.where(jnp.logical_and(k >= 2, k <= nz), 2, 1), own_line, 0
            )

            def other_line(j, x):
                attend(slot(k - 2, j), low, high)
                return x

            lax.fori_loop(1, jnp.where(k >= 2, ny, 1), other_line, 0)
            return inner

        @pl.when(k == 2)
        def _():
            for j in range(1, nb):
                for copy in query_copies(j):
                    copy.wait_recv()

        lax.fori_loop(0, PARTS, turn, 0)

        @pl.when(k < nz)
        def _():
            for j in range(1, ny):
                arrived(slot(k, j), 0)
                along(k, j, 0, start)

        return carry

    for j in range(1, ny):
        arrived(slot(0, j), 0)
        along(0, j, 0, start)
    lax.fori_loop(1, nz + 2, step, 0)

    def finish(i, carry):
        at = pl.ds(pl.multiple_of(i * rows, rows), rows)
        scaled = acc[at, :] / tot[i]
        for c in range(latent // 128):
            xbuf[c, at, :] = scaled[:, c * 128 : (c + 1) * 128]
        lse = top[i] + jnp.log(tot[i])
        flat = jnp.transpose(jnp.broadcast_to(lse, (rows, 128)))
        ssend[i, pl.ds(0, 8), :] = flat[0:8]
        return carry

    lax.fori_loop(0, nb, finish, 0)
    fills[4].wait()
    for h in range(heads):
        x = jnp.concatenate(
            [
                xbuf.at[c][pl.ds(h, nb * tokens, stride=heads), :]
                for c in range(latent // 128)
            ],
            axis=1,
        ).astype(BF16)
        outf[pl.ds(h, nb * tokens, stride=heads), :] = jnp.dot(
            x, wbuf[h], preferred_element_type=F32
        )
    mine = accepted_ref[0]
    for t in range(1, tokens):
        mine = mine + accepted_ref[t]
    count = jnp.full((8, rows), mine, jnp.int32).astype(F32)
    for i in range(nb):
        osend[i] = outf[pl.ds(i * rows, rows), :].astype(BF16)
        ssend[i, pl.ds(8, 8), :] = count

    def result_copies(k):
        to = lax.rem(blk + k, nb)
        return (
            remote(osend.at[to], orecv.at[k - 1], xsend_sem.at[2 * k - 2], xrecv_sem.at[2 * k - 2], blk_peer(k)),
            remote(ssend.at[to], srecv.at[k - 1], xsend_sem.at[2 * k - 1], xrecv_sem.at[2 * k - 1], blk_peer(k)),
        )

    for k in range(1, nb):
        for c in result_copies(k):
            c.start()

    def column(flat):
        return jnp.transpose(jnp.broadcast_to(flat, (128, rows)))

    for k in range(1, nb):
        for c in result_copies(k):
            c.wait_recv()
    lses = [column(ssend[blk, pl.ds(0, 1), :])]
    lses += [column(srecv[k - 1, pl.ds(0, 1), :]) for k in range(1, nb)]
    peak = functools.reduce(jnp.maximum, lses)
    weights = [jnp.exp(v - peak) for v in lses]
    whole = functools.reduce(jnp.add, weights)
    merged = weights[0] * outf[pl.ds(pl.multiple_of(blk * rows, rows), rows), :]
    for k in range(1, nb):
        merged = merged + weights[k] * orecv[k - 1].astype(F32)
    out_ref[...] = (merged / whole).astype(out_ref.dtype)
    for k in range(1, nb):
        count = count + srecv[k - 1, pl.ds(8, 8), :]
    count_ref[0] = jnp.max(count).astype(jnp.int32)

    def drain(k, carry):
        for c in range(PARTS):
            along(k, 0, c, wait_send)
            if c > 0:
                across(k, c, wait_send)
        for j in range(1, ny):
            along(k, j, 0, wait_send)
        return carry

    across(0, 0, wait_send)
    lax.fori_loop(0, nz, drain, 0)
    for k in range(1, nb):
        for c in query_copies(k):
            c.wait_send()
        for c in result_copies(k):
            c.wait_send()


def shards(n_seq, n_blk, q_latent, q_rope, cache_latent, cache_rope, draft_latent, draft_rope,
           ancestors, valid_length, accepted, w_value):
    tokens, heads, latent = q_latent.shape
    rows = tokens * heads
    keys = cache_latent.shape[0]
    ny = inner_extent(n_seq)
    nz = n_seq // ny
    assert keys == latent and (keys + ROPE) % (16 * PARTS) == 0
    query = q_latent.reshape(rows, latent)
    vmem = pl.BlockSpec(memory_space=pltpu.VMEM)
    smem = pl.BlockSpec(memory_space=pltpu.SMEM)
    hbm = pl.BlockSpec(memory_space=pl.ANY)
    dma = pltpu.SemaphoreType.DMA
    out, count = pl.pallas_call(
        functools.partial(kernel, nz, ny, n_blk, tokens, heads),
        out_shape=(
            jax.ShapeDtypeStruct((rows, VDIM), BF16),
            jax.ShapeDtypeStruct((1,), jnp.int32),
        ),
        in_specs=[smem, smem, hbm, hbm, hbm, hbm, vmem, vmem, vmem, hbm],
        out_specs=(vmem, smem),
        scratch_shapes=[
            pltpu.VMEM((n_seq, keys + ROPE, latent), BF16),
            pltpu.VMEM((n_blk, rows, latent), BF16),
            pltpu.VMEM((n_blk, rows, ROPE), BF16),
            pltpu.VMEM((tokens, ROPE, heads), BF16),
            pltpu.VMEM((heads, latent, VDIM), BF16),
            pltpu.VMEM((n_blk, rows, 1), F32),
            pltpu.VMEM((n_blk, rows, 1), F32),
            pltpu.VMEM((n_blk * rows, latent), F32),
            pltpu.VMEM((latent // 128, n_blk * rows, 128), F32),
            pltpu.VMEM((n_blk * rows, VDIM), F32),
            pltpu.VMEM((n_blk, rows, VDIM), BF16),
            pltpu.VMEM((n_blk, 16, rows), F32),
            pltpu.VMEM((n_blk - 1, rows, VDIM), BF16),
            pltpu.VMEM((n_blk - 1, 16, rows), F32),
            dma((5,)),
            dma((2 * (n_blk - 1),)),
            dma((2 * (n_blk - 1),)),
            dma((PARTS * n_seq,)),
            dma((PARTS * n_seq,)),
            dma((PARTS * n_seq,)),
            dma((PARTS * n_seq,)),
            dma((2 * (n_blk - 1),)),
            dma((2 * (n_blk - 1),)),
        ],
        compiler_params=pltpu.CompilerParams(
            collective_id=0, has_side_effects=True, vmem_limit_bytes=60 * 1024 * 1024
        ),
    )(
        valid_length.reshape(1), accepted, query, q_rope, cache_latent, cache_rope,
        draft_latent, draft_rope, ancestors, w_value,
    )
    return (out.reshape(tokens, heads, VDIM), count.reshape(()))


def solution(mesh):
    body = functools.partial(shards, mesh.shape["seq"], mesh.shape["blk"])
    return jax.shard_map(
        body,
        mesh=mesh,
        in_specs=(
            P("blk", "seq", None),
            P("blk", None, "seq"),
            P(("seq", "blk"), None),
            P(None, ("seq", "blk")),
            P(),
            P(),
            P(),
            P(),
            P("blk"),
            P("seq", None, None),
        ),
        out_specs=(P("blk", "seq", None), P()),
        check_vma=False,
    )
```

```python
import functools

import jax
import jax.numpy as jnp
from jax import lax
from jax.experimental import pallas as pl
from jax.experimental.pallas import tpu as pltpu
from jax.sharding import PartitionSpec as P

ROPE = 64
VDIM = 128
PARTS = 6
NEG = -1e30
F32 = jnp.float32
BF16 = jnp.bfloat16
NT = (((1,), (1,)), ((), ()))


def inner_extent(n_seq):
    side = 1
    while 2 * side * side * 4 <= n_seq:
        side *= 2
    return side if n_seq % side == 0 else 1


def kernel(
    nz,
    ny,
    nb,
    tokens,
    heads,
    valid_ref,
    accepted_ref,
    q_ref,
    qr_ref,
    kl_ref,
    kr_ref,
    dl_ref,
    dr_ref,
    anc_ref,
    w_ref,
    out_ref,
    count_ref,
    kbuf,
    qbuf,
    qrbuf,
    wbuf,
    top,
    tot,
    acc,
    xbuf,
    outf,
    osend,
    ssend,
    orecv,
    srecv,
    local_sem,
    qsend_sem,
    qrecv_sem,
    up_sem,
    down_sem,
    side_sem,
    recv_sem,
    xsend_sem,
    xrecv_sem,
):
    scale = (VDIM + ROPE) ** (-0.5)
    rows = tokens * heads
    keys, latent = kl_ref.shape
    seq = lax.axis_index("seq")
    blk = lax.axis_index("blk")
    z, y = seq // ny, seq % ny

    fills = [
        pltpu.make_async_copy(kl_ref, kbuf.at[seq, pl.ds(0, keys)], local_sem.at[0]),
        pltpu.make_async_copy(kr_ref, kbuf.at[seq, pl.ds(keys, ROPE)], local_sem.at[1]),
        pltpu.make_async_copy(q_ref, qbuf.at[blk], local_sem.at[2]),
        pltpu.make_async_copy(qr_ref, qrbuf.at[blk], local_sem.at[3]),
        pltpu.make_async_copy(w_ref, wbuf, local_sem.at[4]),
    ]
    for fill in fills:
        fill.start()

    def blk_peer(k):
        return {"blk": lax.rem(blk + k, nb)}

    def side_peer(j):
        return {"seq": z * ny + lax.rem(y + j, ny)}

    barrier = pltpu.get_barrier_semaphore()
    for k in range(1, nb):
        pl.semaphore_signal(barrier, inc=1, device_id=blk_peer(k))
    for j in range(1, ny):
        pl.semaphore_signal(barrier, inc=1, device_id=side_peer(j))

    @pl.when(z < nz - 1)
    def _():
        pl.semaphore_signal(barrier, inc=1, device_id={"seq": seq + ny})

    @pl.when(z > 0)
    def _():
        pl.semaphore_signal(barrier, inc=1, device_id={"seq": seq - ny})

    arrivals = (nb - 1) + (ny - 1) + jnp.where(z < nz - 1, 1, 0) + jnp.where(z > 0, 1, 0)
    pl.semaphore_wait(barrier, arrivals)

    above, below = nz - 1 - z, z
    near = jnp.minimum(above, below)

    def plane(k):
        odd = lax.rem(k, 2)
        close = jnp.where(odd == 1, z + (k + 1) // 2, z - k // 2)
        far = jnp.where(above > below, z + (k - near), z - (k - near))
        return jnp.where(k <= 2 * near, close, far)

    def remote(src, dst, send, recv, where):
        return pltpu.make_async_remote_copy(
            src_ref=src, dst_ref=dst, send_sem=send, recv_sem=recv,
            device_id=where, device_id_type=pl.DeviceIdType.MESH,
        )

    size = (keys + ROPE) // PARTS

    def slot(k, j):
        return plane(k) * ny + lax.rem(y + j, ny)

    def part(p, c, send, where):
        here = kbuf.at[p, pl.ds(pl.multiple_of(c * size, 16), size)]
        return remote(here, here, send, recv_sem.at[PARTS * p + c], where)

    def arrived(p, c):
        part(p, c, recv_sem.at[PARTS * p + c], {"seq": seq}).wait_recv()

    def along(k, j, c, act):
        index = PARTS * (k * ny + j) + c

        @pl.when(jnp.logical_and(plane(k) <= z, z < nz - 1))
        def _():
            to = {"seq": jnp.minimum(seq + ny, nz * ny - 1)}
            act(part(slot(k, j), c, up_sem.at[index], to))

        @pl.when(jnp.logical_and(plane(k) >= z, z > 0))
        def _():
            to = {"seq": jnp.maximum(seq - ny, 0)}
            act(part(slot(k, j), c, down_sem.at[index], to))

    def across(k, c, act):
        for j in range(1, ny):
            index = PARTS * (k * ny + j) + c
            act(part(slot(k, 0), c, side_sem.at[index], side_peer(j)))

    def start(copy):
        copy.start()

    def wait_send(copy):
        copy.wait_send()

    fills[0].wait()
    fills[1].wait()
    for c in range(PARTS):
        across(0, c, start)
        along(0, 0, c, start)

    def query_copies(k):
        return (
            remote(q_ref, qbuf.at[blk], qsend_sem.at[2 * k - 2], qrecv_sem.at[2 * k - 2], blk_peer(k)),
            remote(qr_ref, qrbuf.at[blk], qsend_sem.at[2 * k - 1], qrecv_sem.at[2 * k - 1], blk_peer(k)),
        )

    for k in range(1, nb):
        for c in query_copies(k):
            c.start()

    top[...] = jnp.full_like(top, NEG)
    tot[...] = jnp.zeros_like(tot)

    def clear(i, carry):
        acc[pl.ds(i * rows, rows), :] = jnp.zeros((rows, latent), F32)
        return carry

    lax.fori_loop(0, nb, clear, 0)
    fills[2].wait()
    fills[3].wait()
    nodes = dl_ref.shape[0]
    dscore = lax.dot_general(qbuf[blk], dl_ref[...], NT, preferred_element_type=F32)
    dscore = dscore + jnp.dot(qrbuf[blk], dr_ref[...], preferred_element_type=F32)
    row = lax.broadcasted_iota(jnp.int32, (rows, tokens), 0)
    first = lax.broadcasted_iota(jnp.int32, (rows, tokens), 1) * heads
    spread = jnp.where(jnp.logical_and(row >= first, row < first + heads), 1.0, 0.0)
    tree = anc_ref[pl.ds(pl.multiple_of(blk * tokens, tokens), tokens), :].astype(F32)
    tree = jnp.dot(spread, tree, preferred_element_type=F32)
    dscore = jnp.where(tree > 0.5, dscore * scale, NEG)
    dpeak = jnp.max(dscore, axis=1, keepdims=True)
    dweight = jnp.exp(dscore - dpeak)
    top[blk] = dpeak
    tot[blk] = jnp.sum(dweight, axis=1, keepdims=True)
    acc[pl.ds(pl.multiple_of(blk * rows, rows), rows), :] = jnp.dot(
        dweight.astype(BF16), dl_ref[...], preferred_element_type=F32
    )
    valid = valid_ref[0]

    def attend(p, low, high):
        first_key = (p * nb + blk) * keys
        live = first_key + lax.broadcasted_iota(jnp.int32, (1, keys), 1) < valid

        def block(i, carry):
            key = kbuf[p, pl.ds(0, keys), :]
            score = lax.dot_general(qbuf[i], key, NT, preferred_element_type=F32)
            score = score + jnp.dot(
                qrbuf[i], kbuf[p, pl.ds(keys, ROPE), :], preferred_element_type=F32
            )
            score = jnp.where(live, score * scale, NEG)
            old = top[i]
            new = jnp.maximum(old, jnp.max(score, axis=1, keepdims=True))
            weight = jnp.exp(score - new)
            fade = jnp.exp(old - new)
            top[i] = new
            tot[i] = tot[i] * fade + jnp.sum(weight, axis=1, keepdims=True)
            at = pl.ds(pl.multiple_of(i * rows, rows), rows)
            acc[at, :] = acc[at, :] * fade + jnp.dot(
                weight.astype(BF16), key, preferred_element_type=F32
            )
            return carry

        lax.fori_loop(low, high, block, 0)

    def step(k, carry):
        def turn(c, inner):
            @pl.when(k < nz)
            def _():
                arrived(slot(k, 0), c)
                along(k, 0, c, start)

                @pl.when(c > 0)
                def _():
                    across(k, c, start)

            low, high = c * nb // PARTS, (c + 1) * nb // PARTS

            @pl.when(jnp.logical_and(k >= 2, c == 0))
            def _():
                for j in range(1, ny):
                    for other in range(1, PARTS):
                        arrived(slot(k - 2, j), other)

            def own_line(n, x):
                attend(slot(jnp.where(n == 0, 0, k - 1), 0), low, high)
                return x

            lax.fori_loop(
                jnp.where(k == 2, 0, 1), jnp.where(jnp.logical_and(k >= 2, k <= nz), 2, 1), own_line, 0
            )

            def other_line(j, x):
                attend(slot(k - 2, j), low, high)
                return x

            lax.fori_loop(1, jnp.where(k >= 2, ny, 1), other_line, 0)
            return inner

        @pl.when(k == 2)
        def _():
            for j in range(1, nb):
                for copy in query_copies(j):
                    copy.wait_recv()

        lax.fori_loop(0, PARTS, turn, 0)

        @pl.when(k < nz)
        def _():
            for j in range(1, ny):
                arrived(slot(k, j), 0)
                along(k, j, 0, start)

        return carry

    for j in range(1, ny):
        arrived(slot(0, j), 0)
        along(0, j, 0, start)
    lax.fori_loop(1, nz + 2, step, 0)

    def finish(i, carry):
        at = pl.ds(pl.multiple_of(i * rows, rows), rows)
        scaled = acc[at, :] / tot[i]
        for c in range(latent // 128):
            xbuf[c, at, :] = scaled[:, c * 128 : (c + 1) * 128]
        lse = top[i] + jnp.log(tot[i])
        flat = jnp.transpose(jnp.broadcast_to(lse, (rows, 128)))
        ssend[i, pl.ds(0, 8), :] = flat[0:8]
        return carry

    lax.fori_loop(0, nb, finish, 0)
    fills[4].wait()
    for h in range(heads):
        x = jnp.concatenate(
            [
                xbuf.at[c][pl.ds(h, nb * tokens, stride=heads), :]
                for c in range(latent // 128)
            ],
            axis=1,
        ).astype(BF16)
        outf[pl.ds(h, nb * tokens, stride=heads), :] = jnp.dot(
            x, wbuf[h], preferred_element_type=F32
        )
    mine = accepted_ref[0]
    for t in range(1, tokens):
        mine = mine + accepted_ref[t]
    count = jnp.full((8, rows), mine, jnp.int32).astype(F32)
    for i in range(nb):
        osend[i] = outf[pl.ds(i * rows, rows), :].astype(BF16)
        ssend[i, pl.ds(8, 8), :] = count

    def result_copies(k):
        to = lax.rem(blk + k, nb)
        return (
            remote(osend.at[to], orecv.at[k - 1], xsend_sem.at[2 * k - 2], xrecv_sem.at[2 * k - 2], blk_peer(k)),
            remote(ssend.at[to], srecv.at[k - 1], xsend_sem.at[2 * k - 1], xrecv_sem.at[2 * k - 1], blk_peer(k)),
        )

    for k in range(1, nb):
        for c in result_copies(k):
            c.start()

    def column(flat):
        return jnp.transpose(jnp.broadcast_to(flat, (128, rows)))

    for k in range(1, nb):
        for c in result_copies(k):
            c.wait_recv()
    lses = [column(ssend[blk, pl.ds(0, 1), :])]
    lses += [column(srecv[k - 1, pl.ds(0, 1), :]) for k in range(1, nb)]
    peak = functools.reduce(jnp.maximum, lses)
    weights = [jnp.exp(v - peak) for v in lses]
    whole = functools.reduce(jnp.add, weights)
    merged = weights[0] * outf[pl.ds(pl.multiple_of(blk * rows, rows), rows), :]
    for k in range(1, nb):
        merged = merged + weights[k] * orecv[k - 1].astype(F32)
    out_ref[...] = (merged / whole).astype(out_ref.dtype)
    for k in range(1, nb):
        count = count + srecv[k - 1, pl.ds(8, 8), :]
    count_ref[0] = jnp.max(count).astype(jnp.int32)

    def drain(k, carry):
        for c in range(PARTS):
            along(k, 0, c, wait_send)
            if c > 0:
                across(k, c, wait_send)
        for j in range(1, ny):
            along(k, j, 0, wait_send)
        return carry

    across(0, 0, wait_send)
    lax.fori_loop(0, nz, drain, 0)
    for k in range(1, nb):
        for c in query_copies(k):
            c.wait_send()
        for c in result_copies(k):
            c.wait_send()


def shards(n_seq, n_blk, q_latent, q_rope, cache_latent, cache_rope, draft_latent, draft_rope,
           ancestors, valid_length, accepted, w_value):
    tokens, heads, latent = q_latent.shape
    rows = tokens * heads
    keys = cache_latent.shape[0]
    ny = inner_extent(n_seq)
    nz = n_seq // ny
    assert keys == latent and (keys + ROPE) % (16 * PARTS) == 0
    query = q_latent.reshape(rows, latent)
    rotary = jnp.transpose(q_rope, (0, 2, 1)).reshape(rows, ROPE)
    vmem = pl.BlockSpec(memory_space=pltpu.VMEM)
    smem = pl.BlockSpec(memory_space=pltpu.SMEM)
    hbm = pl.BlockSpec(memory_space=pl.ANY)
    dma = pltpu.SemaphoreType.DMA
    out, count = pl.pallas_call(
        functools.partial(kernel, nz, ny, n_blk, tokens, heads),
        out_shape=(
            jax.ShapeDtypeStruct((rows, VDIM), BF16),
            jax.ShapeDtypeStruct((1,), jnp.int32),
        ),
        in_specs=[smem, smem, hbm, hbm, hbm, hbm, vmem, vmem, vmem, hbm],
        out_specs=(vmem, smem),
        scratch_shapes=[
            pltpu.VMEM((n_seq, keys + ROPE, latent), BF16),
            pltpu.VMEM((n_blk, rows, latent), BF16),
            pltpu.VMEM((n_blk, rows, ROPE), BF16),
            pltpu.VMEM((heads, latent, VDIM), BF16),
            pltpu.VMEM((n_blk, rows, 1), F32),
            pltpu.VMEM((n_blk, rows, 1), F32),
            pltpu.VMEM((n_blk * rows, latent), F32),
            pltpu.VMEM((latent // 128, n_blk * rows, 128), F32),
            pltpu.VMEM((n_blk * rows, VDIM), F32),
            pltpu.VMEM((n_blk, rows, VDIM), BF16),
            pltpu.VMEM((n_blk, 16, rows), F32),
            pltpu.VMEM((n_blk - 1, rows, VDIM), BF16),
            pltpu.VMEM((n_blk - 1, 16, rows), F32),
            dma((5,)),
            dma((2 * (n_blk - 1),)),
            dma((2 * (n_blk - 1),)),
            dma((PARTS * n_seq,)),
            dma((PARTS * n_seq,)),
            dma((PARTS * n_seq,)),
            dma((PARTS * n_seq,)),
            dma((2 * (n_blk - 1),)),
            dma((2 * (n_blk - 1),)),
        ],
        compiler_params=pltpu.CompilerParams(
            collective_id=0, has_side_effects=True, vmem_limit_bytes=60 * 1024 * 1024
        ),
    )(
        valid_length.reshape(1), accepted, query, rotary, cache_latent, cache_rope,
        draft_latent, draft_rope, ancestors, w_value,
    )
    return (out.reshape(tokens, heads, VDIM), count.reshape(()))


def solution(mesh):
    body = functools.partial(shards, mesh.shape["seq"], mesh.shape["blk"])
    return jax.shard_map(
        body,
        mesh=mesh,
        in_specs=(
            P("blk", "seq", None),
            P("blk", None, "seq"),
            P(("seq", "blk"), None),
            P(None, ("seq", "blk")),
            P(),
            P(),
            P(),
            P(),
            P("blk"),
            P("seq", None, None),
        ),
        out_specs=(P("blk", "seq", None), P()),
        check_vma=False,
    )
```
